32 devices in a mesh: left: 8 (over y, x, core), right: 4 (over z).
Axes of the slice: x: 2, y: 2, z: 4, core: 2. Of those that a mesh axis runs over, the one named last changes fastest.
Arguments:
- left_freq: float32 [16384], P('left'), as said below
- right_freq: float32 [16384], P('right'), as said below
- left_dirs: float32 [16, 16384], P(None, 'left'), may hold values from -6 to 6
- left_data: float32 [16, 16384], P(None, 'left'), may hold values from -6 to 6
- right_dirs: float32 [16, 16384], P(None, 'right'), may hold values from -6 to 6
- right_data: float32 [16, 16384], P(None, 'right'), may hold values from -6 to 6
- col_sketch: bfloat16 [16384, 256], P('right'), may hold values from -0.047265625 to 0.047265625
- row_sketch: bfloat16 [16384, 256], P('left'), may hold values from -0.047265625 to 0.047265625
Outputs:
- row_scaled: float32 [16384, 256], P(('left', 'right'))
- col_scaled: float32 [16384, 256], P('right')
- lower_reduced: float32 [256, 256], replicated
- shifted_reduced: float32 [256, 256], replicated
The draws below stay inside these ranges and needn't reach their ends.
Inputs may be any that keep to these rules, and one draw needn't show every extreme that they name: left_freq[i] = 1 + (k + e) / 16384 with k distinct whole numbers of 0 to 16383 and |e| at most 0.2. right_freq[j] = 1 + (k + 0.5 + e) / 16384 with k distinct whole numbers of 0 to 16383 and |e| at most 0.2; left and right frequencies share the spacing 1 / 16384, so every left and right frequency differ by 0.1 / 16384 or more.
All inputs are finite; a program needn't handle non-finite values.
Results may differ from the reference program's by a relative error of at most 0.0089.
Values sent between devices are 32-bit elements; how exact they have to be, the bound alone decides.
A program may use at most 256 MiB of HBM per device.

```python
import math
import jax
import jax.numpy as jnp
from jax import lax

ROWS_DEV = 2048
SKETCH = 256
PORTS = 16
COLS_DEV = 4096
NR = 16384
NC = 16384


def jitter_values(key, count):
    return jax.random.uniform(key, (count,), jnp.float32, -0.15, 0.15)


def draw_left_freq(key, part):
    own_key = jax.random.fold_in(key, 31)
    index_all = jnp.arange(NR, dtype=jnp.int32)
    slots = NR // ROWS_DEV
    grid_pos = index_all % ROWS_DEV * slots + index_all // ROWS_DEV
    jitter = jitter_values(own_key, NR)
    return (1.0 + (grid_pos.astype(jnp.float32) + jitter) / NR).astype(jnp.float32)


def draw_right_freq(key, part):
    own_key = jax.random.fold_in(key, 57)
    index_all = jnp.arange(NC, dtype=jnp.int32)
    slots = NC // COLS_DEV
    grid_pos = index_all % COLS_DEV * slots + index_all // COLS_DEV
    jitter = jitter_values(own_key, NC)
    return (1.0 + (grid_pos.astype(jnp.float32) + 0.5 + jitter) / NR).astype(jnp.float32)


def sketch_values(key, row_total):
    base_key = jax.random.fold_in(key, 11)
    order_key = jax.random.fold_in(key, 12)
    marks_key = jax.random.fold_in(key, 13)
    signs_key = jax.random.fold_in(key, 14)
    inverse_root = float(row_total) ** (-0.5)
    base = jnp.clip(jax.random.normal(base_key, (row_total, SKETCH), jnp.float32), -6.0, 6.0) * inverse_root
    spread = inverse_root
    pair_count = SKETCH // 4
    order = jax.random.permutation(order_key, SKETCH).astype(jnp.int32)
    rank = jnp.argsort(order).astype(jnp.int32)
    pair_index = rank % pair_count
    is_copy = (rank >= pair_count) & (rank < 2 * pair_count)
    is_paired = rank < 2 * pair_count
    source = jnp.where(is_copy, order[pair_index], jnp.arange(SKETCH, dtype=jnp.int32)).astype(jnp.int32)
    picks = jax.random.randint(marks_key, (row_total, pair_count), 0, 16, dtype=jnp.int32) == 0
    marked = picks[:, pair_index] & is_paired[None, :]
    signs = (jax.random.randint(signs_key, (row_total, SKETCH), 0, 2, dtype=jnp.int32) * 2 - 1).astype(jnp.float32)
    small_step = 0.0016 * spread
    copied = base[:, source]
    values = jnp.where(marked, jnp.where(is_copy[None, :], small_step * signs, 0.0), copied)
    return values.astype(jnp.bfloat16)


def draw_col_sketch(key, part):
    return sketch_values(jax.random.fold_in(key, 71), NC)


def draw_row_sketch(key, part):
    return sketch_values(jax.random.fold_in(key, 73), NR)


def steps_of(rng, shape, split, low, top_value):
    def one(dim, blocks):
        heights = jax.random.uniform(jax.random.fold_in(jax.random.fold_in(rng, 6), dim), (blocks,), jnp.float32, low / len(split), top_value / len(split))
        return jnp.repeat(jnp.exp(heights), shape[dim] // blocks).reshape((-1,) + (1,) * (len(shape) - dim - 1))

    gain = one(*split[0])
    for cut in split[1:]:
        gain = gain * one(*cut)
    return gain


def gaussian(rng, dims, deviation, reach, pieces=(), kind=jnp.bfloat16):
    loudness = steps_of(rng, dims, pieces, -0.22, 0.18) if pieces else 1.0
    drawn = jax.random.normal(rng, dims, jnp.float32) * deviation * loudness
    return jnp.minimum(jnp.maximum(drawn, -reach), reach).astype(kind)


def setup_inputs(seed: int = 0) -> dict:
    key_list = jax.random.split(jax.random.key(seed), 9)
    return {
        "left_freq": draw_left_freq(jax.random.fold_in(key_list[8], 71), 0),
        "right_freq": draw_right_freq(jax.random.fold_in(key_list[8], 71), 0),
        "left_dirs": gaussian(key_list[2], (PORTS, NR), 1.0, 6.0, ((1, 8),), jnp.float32),
        "left_data": gaussian(key_list[3], (PORTS, NR), 1.0, 6.0, ((1, 8),), jnp.float32),
        "right_dirs": gaussian(key_list[4], (PORTS, NC), 1.0, 6.0, ((1, 4),), jnp.float32),
        "right_data": gaussian(key_list[5], (PORTS, NC), 1.0, 6.0, ((1, 4),), jnp.float32),
        "col_sketch": draw_col_sketch(jax.random.fold_in(key_list[8], 71), 0),
        "row_sketch": draw_row_sketch(jax.random.fold_in(key_list[8], 71), 0),
    }


precise = lax.Precision.HIGHEST

def build_tiles(freq_rows, dirs_rows, data_rows, right_freq, right_dirs, right_data, total_rows):
    direct = lax.dot_general(data_rows.astype(jnp.float32), right_dirs.astype(jnp.float32), (((0,), (0,)), ((), ())), precision=precise, preferred_element_type=jnp.float32)
    crossed = lax.dot_general(dirs_rows.astype(jnp.float32), right_data.astype(jnp.float32), (((0,), (0,)), ((), ())), precision=precise, preferred_element_type=jnp.float32)
    spacing_gap = total_rows * (freq_rows[:, None] - right_freq[None, :])
    lower_tile = ((direct - crossed) / spacing_gap).astype(jnp.bfloat16)
    shift_tile = ((freq_rows[:, None] * direct - right_freq[None, :] * crossed) / spacing_gap).astype(jnp.bfloat16)
    return (lower_tile, shift_tile)

def factor_pass(basis, shifted_flag):
    gram_sum = lax.dot_general(basis.astype(jnp.float32), basis.astype(jnp.float32), (((0,), (0,)), ((), ())), precision=precise, preferred_element_type=jnp.float32)
    width = gram_sum.shape[0]
    identity = jnp.eye(width, dtype=jnp.float32)
    if shifted_flag:
        gram_sum = gram_sum + 1e-05 * jnp.trace(gram_sum) / width * identity
    factor = jnp.linalg.cholesky(gram_sum)
    inverse = jax.scipy.linalg.solve_triangular(factor, identity, lower=True)
    return lax.dot_general(basis.astype(jnp.float32), inverse.astype(jnp.float32), (((1,), (1,)), ((), ())), precision=precise, preferred_element_type=jnp.float32)

def orthonormalize(image):
    return factor_pass(factor_pass(image, True), False)

def reference(left_freq, right_freq, left_dirs, left_data, right_dirs, right_data, col_sketch, row_sketch):
    blocks = NR // ROWS_DEV
    freq_blocks = left_freq.reshape(blocks, ROWS_DEV)
    dirs_blocks = left_dirs.reshape(PORTS, blocks, ROWS_DEV).transpose(1, 0, 2)
    data_blocks = left_data.reshape(PORTS, blocks, ROWS_DEV).transpose(1, 0, 2)
    sketch_blocks = row_sketch.reshape(blocks, ROWS_DEV, SKETCH)

    def first_sweep(running, block_in):
        freq_rows, dirs_rows, data_rows, sketch_rows = block_in
        lower_tile, shift_tile = build_tiles(freq_rows, dirs_rows, data_rows, right_freq, right_dirs, right_data, NR)
        rows_out = jnp.dot(lower_tile.astype(jnp.float32), col_sketch.astype(jnp.float32), preferred_element_type=jnp.float32)
        running = running + lax.dot_general(lower_tile.astype(jnp.float32), sketch_rows.astype(jnp.float32), (((0,), (0,)), ((), ())), preferred_element_type=jnp.float32)
        return (running, rows_out)
    col_image, row_blocks = lax.scan(first_sweep, jnp.zeros((NC, SKETCH), jnp.float32), (freq_blocks, dirs_blocks, data_blocks, sketch_blocks))
    row_image = row_blocks.reshape(NR, SKETCH)
    row_basis = orthonormalize(row_image)
    col_basis = orthonormalize(col_image)
    col_round = col_basis.astype(jnp.bfloat16)
    basis_blocks = row_basis.reshape(blocks, ROWS_DEV, SKETCH)

    def second_sweep(running, block_in):
        freq_rows, dirs_rows, data_rows, basis_rows = block_in
        lower_tile, shift_tile = build_tiles(freq_rows, dirs_rows, data_rows, right_freq, right_dirs, right_data, NR)
        lower_applied = jnp.dot(lower_tile.astype(jnp.float32), col_round.astype(jnp.float32), preferred_element_type=jnp.float32)
        shift_applied = jnp.dot(shift_tile.astype(jnp.float32), col_round.astype(jnp.float32), preferred_element_type=jnp.float32)
        lower_part = lax.dot_general(basis_rows.astype(jnp.float32), lower_applied.astype(jnp.float32), (((0,), (0,)), ((), ())), precision=precise, preferred_element_type=jnp.float32)
        shift_part = lax.dot_general(basis_rows.astype(jnp.float32), shift_applied.astype(jnp.float32), (((0,), (0,)), ((), ())), precision=precise, preferred_element_type=jnp.float32)
        return ((running[0] + lower_part, running[1] + shift_part), None)
    start_sums = (jnp.zeros((SKETCH, SKETCH), jnp.float32), jnp.zeros((SKETCH, SKETCH), jnp.float32))
    reduced_pair, unused_out = lax.scan(second_sweep, start_sums, (freq_blocks, dirs_blocks, data_blocks, basis_blocks))
    return (row_basis * math.sqrt(NR), col_basis * math.sqrt(NC), reduced_pair[0], reduced_pair[1])
```

```python
import functools
import math

import jax
import jax.numpy as jnp
from jax import lax
from jax.experimental import pallas as pl
from jax.experimental.pallas import tpu as pltpu
from jax.sharding import PartitionSpec as P

precise = lax.Precision.HIGHEST
F32 = jnp.float32
BF16 = jnp.bfloat16
LEFT_PARTS = (0, 0, 1, 0, 1, 2)
RIGHT_PARTS = (0, 1, 0, 2, 1, 0)


def tdot(a, b, precision=None):
    return lax.dot_general(
        a, b, (((0,), (0,)), ((), ())), precision=precision, preferred_element_type=F32
    )


def split3(x):
    one = x.astype(BF16).astype(F32)
    rest = x - one
    two = rest.astype(BF16).astype(F32)
    return (one, two, (rest - two).astype(BF16).astype(F32))


def stack_parts(first, second, order):
    a, b = split3(first), split3(second)
    pieces = [a[p] for p in order] + [b[p] for p in order]
    pad = jnp.zeros((256 - 12 * first.shape[0], first.shape[1]), F32)
    return jnp.concatenate(pieces + [pad], axis=0)


def tile_kernel(
    total, rows_step,
    lf_ref, rf_ref, ld_ref, la_ref, rd_ref, ra_ref, cs_ref, rs_ref,
    tile_ref, row_ref, col_ref,
    left_scr, sketch_scr,
):
    step = pl.program_id(0)
    rows = left_scr.shape[0]

    @pl.when(step == 0)
    def _():
        for r in range(0, rows, 512):
            stacked = stack_parts(la_ref[:, r:r + 512], -ld_ref[:, r:r + 512], LEFT_PARTS)
            left_scr[r:r + 512, :] = stacked.T.astype(BF16)
            sketch_scr[:, r:r + 512] = rs_ref[r:r + 512, :].astype(F32).T.astype(BF16)
        row_ref[...] = jnp.zeros_like(row_ref)

    right = stack_parts(rd_ref[...], ra_ref[...], RIGHT_PARTS).astype(BF16)
    freq = rf_ref[...]
    acc = jnp.zeros((256, right.shape[1]), F32)
    for chunk in range(rows // rows_step):
        sl = pl.ds(chunk * rows_step, rows_step)
        numer = jnp.dot(left_scr[sl, :], right, preferred_element_type=F32)
        gap = total * (lf_ref[sl, :] - freq)
        tile = (numer / gap).astype(BF16)
        tile_ref[sl, :] = tile
        row_ref[sl, :] += jnp.dot(tile, cs_ref[...], preferred_element_type=F32)
        acc += jnp.dot(sketch_scr[:, sl], tile, preferred_element_type=F32)
    col_ref[...] = acc.T


def build(lf, rf, ld, la, rd, ra, cs, rs, total):
    rows, cols = lf.shape[0], rf.shape[0]
    ports, width = ld.shape[0], cs.shape[1]
    tc = 256
    fixed = lambda j: (0, 0)
    return pl.pallas_call(
        functools.partial(tile_kernel, float(total), 256),
        grid=(cols // tc,),
        in_specs=[
            pl.BlockSpec((rows, 1), fixed),
            pl.BlockSpec((1, tc), lambda j: (0, j)),
            pl.BlockSpec((ports, rows), fixed),
            pl.BlockSpec((ports, rows), fixed),
            pl.BlockSpec((ports, tc), lambda j: (0, j)),
            pl.BlockSpec((ports, tc), lambda j: (0, j)),
            pl.BlockSpec((tc, width), lambda j: (j, 0)),
            pl.BlockSpec((rows, width), fixed),
        ],
        out_specs=[
            pl.BlockSpec((rows, tc), lambda j: (0, j)),
            pl.BlockSpec((rows, width), fixed),
            pl.BlockSpec((tc, width), lambda j: (j, 0)),
        ],
        out_shape=[
            jax.ShapeDtypeStruct((rows, cols), BF16),
            jax.ShapeDtypeStruct((rows, width), F32),
            jax.ShapeDtypeStruct((cols, width), F32),
        ],
        scratch_shapes=[pltpu.VMEM((rows, 256), BF16), pltpu.VMEM((width, rows), BF16)],
        compiler_params=pltpu.CompilerParams(
            dimension_semantics=("arbitrary",), vmem_limit_bytes=40 << 20
        ),
        name="tiles",
    )(lf[:, None], rf[None, :], ld, la, rd, ra, cs, rs)


BLOCK = 32


def chol_kernel(shifted, g_ref, out_ref, work):
    width = g_ref.shape[-1]
    row_id = lax.broadcasted_iota(jnp.int32, (width, width), 0)
    col_id = lax.broadcasted_iota(jnp.int32, (width, width), 1)
    eye = (row_id == col_id).astype(F32)
    for m in range(2):
        gram = g_ref[m]
        if shifted:
            trace = jnp.sum(jnp.sum(gram * eye, axis=1, keepdims=True), axis=0, keepdims=True)
            gram = gram + (1e-05 * trace / width) * eye
        work[m, :, 0:width] = gram
        work[m, :, width:] = eye
    brow = lax.broadcasted_iota(jnp.int32, (BLOCK, BLOCK), 0)
    bcol = lax.broadcasted_iota(jnp.int32, (BLOCK, BLOCK), 1)
    small_eye = (brow == bcol).astype(F32)
    for k in range(0, width, BLOCK):
        for m in range(2):
            block = work[m, k:k + BLOCK, k:k + BLOCK]
            pair = jnp.concatenate([block, small_eye], axis=1)
            low = lax.broadcasted_iota(jnp.int32, pair.shape, 0)
            scale = jnp.ones((BLOCK, 1), F32)
            for s in range(BLOCK):
                pivot = pair[s:s + 1, :]
                top = 1.0 / pair[s:s + 1, s:s + 1]
                column = jnp.where(low > s, pair[:, s:s + 1], 0.0)
                pair = pair - column * (pivot * top)
            diag = jnp.sum(pair[:, 0:BLOCK] * small_eye, axis=1, keepdims=True)
            inv = pair[:, BLOCK:] * lax.rsqrt(diag)
            rows = jnp.dot(
                inv, work[m, k:k + BLOCK, :], precision=precise, preferred_element_type=F32
            )
            out_ref[m, k:k + BLOCK, :] = rows[:, width:]
            if k + BLOCK < width:
                lo = k + BLOCK
                work[m, lo:, :] = work[m, lo:, :] - tdot(rows[:, lo:width], rows, precise)


def chol_inverse(grams, shifted):
    width = grams.shape[-1]
    return pl.pallas_call(
        functools.partial(chol_kernel, shifted),
        in_specs=[pl.BlockSpec(memory_space=pltpu.VMEM)],
        out_specs=pl.BlockSpec(memory_space=pltpu.VMEM),
        out_shape=jax.ShapeDtypeStruct((2, width, width), F32),
        scratch_shapes=[pltpu.VMEM((2, width, 2 * width), F32)],
        compiler_params=pltpu.CompilerParams(vmem_limit_bytes=32 << 20),
        name="factor",
    )(grams)


def apply_inverse(basis, inverse):
    return lax.dot_general(
        basis, inverse, (((1,), (1,)), ((), ())), precision=precise, preferred_element_type=F32
    )


def body(lf, rf, ld, la, rd, ra, cs, rs):
    rows, cols = lf.shape[0], rf.shape[0]
    left_n, right_n = lax.axis_size("left"), lax.axis_size("right")
    total_rows, total_cols = rows * left_n, cols * right_n
    tile, row_full, col_full = build(lf, rf, ld, la, rd, ra, cs, rs, total_rows)
    row_full = lax.psum(row_full, "right")
    col_full = lax.psum(col_full, "left")
    for sweep in range(2):
        gram_rows = lax.psum(tdot(row_full, row_full, precise), "left")
        gram_cols = lax.psum(tdot(col_full, col_full, precise), "right")
        inverse = chol_inverse(jnp.stack([gram_rows, gram_cols]), sweep == 0)
        row_full = apply_inverse(row_full, inverse[0])
        col_full = apply_inverse(col_full, inverse[1])
    share = rows // right_n
    row_part = lax.dynamic_slice_in_dim(row_full, lax.axis_index("right") * share, share, 0)
    col_round = col_full.astype(BF16)
    applied = jnp.dot(tile, col_round, preferred_element_type=F32)
    both = jnp.concatenate([applied, applied * lf[:, None]], axis=1)
    reduced = tdot(row_full, both, precise)
    low_rank = jnp.dot(
        lax.dot_general(row_full, ld, (((0,), (1,)), ((), ())), precision=precise),
        jnp.dot(ra, col_round.astype(F32), precision=precise) * (1.0 / total_rows),
        precision=precise,
    )
    width = cs.shape[1]
    reduced = jnp.concatenate([reduced[:, :width], reduced[:, width:] + low_rank], axis=1)
    reduced = lax.psum(reduced, ("left", "right"))
    return (
        row_part * math.sqrt(total_rows),
        col_full * math.sqrt(total_cols),
        reduced[:, :width],
        reduced[:, width:],
    )


def solution(mesh):
    in_specs = (
        P("left"), P("right"), P(None, "left"), P(None, "left"),
        P(None, "right"), P(None, "right"), P("right", None), P("left", None),
    )
    out_specs = (P(("left", "right"), None), P("right", None), P(), P())
    return jax.shard_map(body, mesh=mesh, in_specs=in_specs, out_specs=out_specs, check_vma=False)
```

```python
import functools
import math

import jax
import jax.numpy as jnp
from jax import lax
from jax.experimental import pallas as pl
from jax.experimental.pallas import tpu as pltpu
from jax.sharding import PartitionSpec as P

precise = lax.Precision.HIGHEST
F32 = jnp.float32
BF16 = jnp.bfloat16
LEFT_PARTS = (0, 0, 1, 0, 1, 2)
RIGHT_PARTS = (0, 1, 0, 2, 1, 0)


def tdot(a, b, precision=None):
    return lax.dot_general(
        a, b, (((0,), (0,)), ((), ())), precision=precision, preferred_element_type=F32
    )


def split3(x):
    one = x.astype(BF16).astype(F32)
    rest = x - one
    two = rest.astype(BF16).astype(F32)
    return (one, two, (rest - two).astype(BF16).astype(F32))


def stack_parts(first, second, order):
    a, b = split3(first), split3(second)
    pieces = [a[p] for p in order] + [b[p] for p in order]
    pad = jnp.zeros((256 - 12 * first.shape[0], first.shape[1]), F32)
    return jnp.concatenate(pieces + [pad], axis=0)


def tile_kernel(
    total, rows_step,
    lf_ref, rf_ref, ld_ref, la_ref, rd_ref, ra_ref, cs_ref, rs_ref,
    tile_ref, row_ref, col_ref,
    left_scr, sketch_scr,
):
    step = pl.program_id(0)
    rows = left_scr.shape[0]

    @pl.when(step == 0)
    def _():
        for r in range(0, rows, 512):
            stacked = stack_parts(la_ref[:, r:r + 512], -ld_ref[:, r:r + 512], LEFT_PARTS)
            left_scr[r:r + 512, :] = stacked.T.astype(BF16)
            sketch_scr[:, r:r + 512] = rs_ref[r:r + 512, :].astype(F32).T.astype(BF16)
        row_ref[...] = jnp.zeros_like(row_ref)

    right = stack_parts(rd_ref[...], ra_ref[...], RIGHT_PARTS).astype(BF16)
    freq = rf_ref[...]
    acc = jnp.zeros((256, right.shape[1]), F32)
    for chunk in range(rows // rows_step):
        sl = pl.ds(chunk * rows_step, rows_step)
        numer = jnp.dot(left_scr[sl, :], right, preferred_element_type=F32)
        gap = total * (lf_ref[sl, :] - freq)
        tile = (numer / gap).astype(BF16)
        tile_ref[sl, :] = tile
        row_ref[sl, :] += jnp.dot(tile, cs_ref[...], preferred_element_type=F32)
        acc += jnp.dot(sketch_scr[:, sl], tile, preferred_element_type=F32)
    col_ref[...] = acc.T


def build(lf, rf, ld, la, rd, ra, cs, rs, total):
    rows, cols = lf.shape[0], rf.shape[0]
    ports, width = ld.shape[0], cs.shape[1]
    tc = 256
    fixed = lambda j: (0, 0)
    return pl.pallas_call(
        functools.partial(tile_kernel, float(total), 256),
        grid=(cols // tc,),
        in_specs=[
            pl.BlockSpec((rows, 1), fixed),
            pl.BlockSpec((1, tc), lambda j: (0, j)),
            pl.BlockSpec((ports, rows), fixed),
            pl.BlockSpec((ports, rows), fixed),
            pl.BlockSpec((ports, tc), lambda j: (0, j)),
            pl.BlockSpec((ports, tc), lambda j: (0, j)),
            pl.BlockSpec((tc, width), lambda j: (j, 0)),
            pl.BlockSpec((rows, width), fixed),
        ],
        out_specs=[
            pl.BlockSpec((rows, tc), lambda j: (0, j)),
            pl.BlockSpec((rows, width), fixed),
            pl.BlockSpec((tc, width), lambda j: (j, 0)),
        ],
        out_shape=[
            jax.ShapeDtypeStruct((rows, cols), BF16),
            jax.ShapeDtypeStruct((rows, width), F32),
            jax.ShapeDtypeStruct((cols, width), F32),
        ],
        scratch_shapes=[pltpu.VMEM((rows, 256), BF16), pltpu.VMEM((width, rows), BF16)],
        compiler_params=pltpu.CompilerParams(
            dimension_semantics=("arbitrary",), vmem_limit_bytes=40 << 20
        ),
        name="tiles",
    )(lf[:, None], rf[None, :], ld, la, rd, ra, cs, rs)


BLOCK = 32


def chol_kernel(shifted, g_ref, out_ref, work):
    width = g_ref.shape[-1]
    row_id = lax.broadcasted_iota(jnp.int32, (width, width), 0)
    col_id = lax.broadcasted_iota(jnp.int32, (width, width), 1)
    eye = (row_id == col_id).astype(F32)
    for m in range(2):
        gram = g_ref[m]
        if shifted:
            trace = jnp.sum(jnp.sum(gram * eye, axis=1, keepdims=True), axis=0, keepdims=True)
            gram = gram + (1e-05 * trace / width) * eye
        work[m, :, 0:width] = gram
        work[m, :, width:] = eye
    brow = lax.broadcasted_iota(jnp.int32, (BLOCK, BLOCK), 0)
    bcol = lax.broadcasted_iota(jnp.int32, (BLOCK, BLOCK), 1)
    small_eye = (brow == bcol).astype(F32)
    for k in range(0, width, BLOCK):
        for m in range(2):
            block = work[m, k:k + BLOCK, k:k + BLOCK]
            pair = jnp.concatenate([block, small_eye], axis=1)
            low = lax.broadcasted_iota(jnp.int32, pair.shape, 0)
            scale = jnp.ones((BLOCK, 1), F32)
            for s in range(BLOCK):
                pivot = pair[s:s + 1, :]
                top = 1.0 / pair[s:s + 1, s:s + 1]
                column = jnp.where(low > s, pair[:, s:s + 1], 0.0)
                pair = pair - column * (pivot * top)
            diag = jnp.sum(pair[:, 0:BLOCK] * small_eye, axis=1, keepdims=True)
            inv = pair[:, BLOCK:] * lax.rsqrt(diag)
            rows = jnp.dot(
                inv, work[m, k:k + BLOCK, :], precision=precise, preferred_element_type=F32
            )
            out_ref[m, k:k + BLOCK, :] = rows[:, width:]
            if k + BLOCK < width:
                lo = k + BLOCK
                work[m, lo:, :] = work[m, lo:, :] - tdot(rows[:, lo:width], rows, precise)


def chol_inverse(grams, shifted):
    width = grams.shape[-1]
    return pl.pallas_call(
        functools.partial(chol_kernel, shifted),
        in_specs=[pl.BlockSpec(memory_space=pltpu.VMEM)],
        out_specs=pl.BlockSpec(memory_space=pltpu.VMEM),
        out_shape=jax.ShapeDtypeStruct((2, width, width), F32),
        scratch_shapes=[pltpu.VMEM((2, width, 2 * width), F32)],
        compiler_params=pltpu.CompilerParams(vmem_limit_bytes=32 << 20),
        name="factor",
    )(grams)


def apply_inverse(basis, inverse, precision):
    return lax.dot_general(
        basis, inverse, (((1,), (1,)), ((), ())), precision=precision, preferred_element_type=F32
    )


def places():
    me, deep = lax.axis_index("left"), lax.axis_index("right")
    core = lax.rem(me, 2)
    return me, deep, core, me // 2


def chip_peer(chip, core, offset, chips):
    return {"left": lax.rem(chip + offset, chips) * 2 + core}


def greet(chips, deeps):
    me, deep, core, chip = places()
    barrier = pltpu.get_barrier_semaphore()
    peers = [{"left": chip * 2 + (1 - core)}]
    peers += [chip_peer(chip, core, o, chips) for o in range(1, chips)]
    peers += [{"right": lax.rem(deep + o, deeps)} for o in range(1, deeps)]
    for peer in peers:
        pl.semaphore_signal(
            barrier, inc=1, device_id=peer, device_id_type=pl.DeviceIdType.MESH
        )
    pl.semaphore_wait(barrier, len(peers))


def send(src, dst, sems, slot, peer):
    copy = pltpu.make_async_remote_copy(
        src_ref=src,
        dst_ref=dst,
        send_sem=sems.at[0, slot],
        recv_sem=sems.at[1, slot],
        device_id=peer,
        device_id_type=pl.DeviceIdType.MESH,
    )
    copy.start()
    return copy


def scatter_kernel(
    chips, deeps, row_ref, col_ref, row_out, col_out,
    deep_buf, core_buf, half_buf, chip_buf, deep_sem, core_sem, chip_sem,
):
    me, deep, core, chip = places()
    greet(chips, deeps)
    share, half, piece = row_out.shape[0], core_buf.shape[0], col_out.shape[0]
    pair = send(
        col_ref.at[pl.ds((1 - core) * half, half)], core_buf, core_sem, 0,
        {"left": chip * 2 + (1 - core)},
    )
    deep_copies = []
    for o in range(1, deeps):
        peer = lax.rem(deep + o, deeps)
        deep_copies.append(
            send(
                row_ref.at[pl.ds(peer * share, share)], deep_buf.at[o - 1], deep_sem, o - 1,
                {"right": peer},
            )
        )
    pair.wait()

    @pl.loop(0, chips)
    def _(p):
        sl = pl.ds(p * piece, piece)
        half_buf[sl, :] = col_ref[pl.ds(core * half + p * piece, piece), :] + core_buf[sl, :]

    chip_copies = []
    for o in range(1, chips):
        peer = lax.rem(chip + o, chips)
        chip_copies.append(
            send(
                half_buf.at[pl.ds(peer * piece, piece)], chip_buf.at[o - 1], chip_sem, o - 1,
                {"left": peer * 2 + core},
            )
        )
    col_out[...] = half_buf[pl.ds(chip * piece, piece), :]
    row_out[...] = row_ref[pl.ds(deep * share, share), :]
    for o in range(1, chips):
        chip_copies[o - 1].wait()
        col_out[...] += chip_buf[o - 1]
    for o in range(1, deeps):
        deep_copies[o - 1].wait()
        row_out[...] += deep_buf[o - 1]


def vmem_specs(n):
    return [pl.BlockSpec(memory_space=pltpu.VMEM)] * n


def sem_pair(n):
    return pltpu.SemaphoreType.DMA((2, n))


def comm_params(cid):
    return pltpu.CompilerParams(
        collective_id=cid, has_side_effects=True, vmem_limit_bytes=40 << 20
    )


def scatter(row_image, col_image):
    chips, deeps = lax.axis_size("left") // 2, lax.axis_size("right")
    rows, width = row_image.shape
    cols = col_image.shape[0]
    share, half, piece = rows // deeps, cols // 2, cols // 2 // chips
    return pl.pallas_call(
        functools.partial(scatter_kernel, chips, deeps),
        in_specs=vmem_specs(2),
        out_specs=vmem_specs(2),
        out_shape=[
            jax.ShapeDtypeStruct((share, width), F32),
            jax.ShapeDtypeStruct((piece, width), F32),
        ],
        scratch_shapes=[
            pltpu.VMEM((deeps - 1, share, width), F32),
            pltpu.VMEM((half, width), F32),
            pltpu.VMEM((half, width), F32),
            pltpu.VMEM((chips - 1, piece, width), F32),
            sem_pair(deeps - 1), sem_pair(1), sem_pair(chips - 1),
        ],
        compiler_params=comm_params(1),
        name="scatter",
    )(row_image, col_image)


def reduce_kernel(
    chips, deeps, x_ref, out_ref,
    core_buf, half_buf, chip_buf, deep_buf,
    core_sem, chip_sem, deep_sem, back_sem, last_sem,
):
    me, deep, core, chip = places()
    greet(chips, deeps)
    half, piece = core_buf.shape[0], chip_buf.shape[1]
    sibling = {"left": chip * 2 + (1 - core)}
    send(x_ref.at[pl.ds((1 - core) * half, half)], core_buf, core_sem, 0, sibling).wait()
    half_buf[...] = x_ref[pl.ds(core * half, half), :] + core_buf[...]
    copies = []
    for o in range(1, chips):
        peer = lax.rem(chip + o, chips)
        copies.append(
            send(
                half_buf.at[pl.ds(peer * piece, piece)], chip_buf.at[o - 1], chip_sem, o - 1,
                {"left": peer * 2 + core},
            )
        )
    part = half_buf[pl.ds(chip * piece, piece), :]
    for o in range(1, chips):
        copies[o - 1].wait()
        part = part + chip_buf[o - 1]
    deep_buf[deep] = part
    copies = []
    for o in range(1, deeps):
        copies.append(
            send(
                deep_buf.at[deep], deep_buf.at[deep], deep_sem, o - 1,
                {"right": lax.rem(deep + o, deeps)},
            )
        )
    for copy in copies:
        copy.wait()
    part = deep_buf[0]
    for d in range(1, deeps):
        part = part + deep_buf[d]
    mine = pl.ds(core * half + chip * piece, piece)
    out_ref[mine, :] = part
    copies = []
    for o in range(1, chips):
        copies.append(
            send(
                out_ref.at[mine], out_ref.at[mine], back_sem, o - 1,
                chip_peer(chip, core, o, chips),
            )
        )
    for copy in copies:
        copy.wait()
    own = pl.ds(core * half, half)
    send(out_ref.at[own], out_ref.at[own], last_sem, 0, sibling).wait()


def reduce_all(x, cid):
    chips, deeps = lax.axis_size("left") // 2, lax.axis_size("right")
    rows, width = x.shape
    half, piece = rows // 2, rows // 2 // chips
    return pl.pallas_call(
        functools.partial(reduce_kernel, chips, deeps),
        in_specs=vmem_specs(1),
        out_specs=vmem_specs(1)[0],
        out_shape=jax.ShapeDtypeStruct(x.shape, F32),
        scratch_shapes=[
            pltpu.VMEM((half, width), F32),
            pltpu.VMEM((half, width), F32),
            pltpu.VMEM((chips - 1, piece, width), F32),
            pltpu.VMEM((deeps, piece, width), F32),
            sem_pair(1), sem_pair(chips - 1), sem_pair(deeps - 1), sem_pair(chips - 1),
            sem_pair(1),
        ],
        compiler_params=comm_params(cid),
        name="reduce",
    )(x)


def gather_kernel(
    chips, deeps, row_ref, col_ref, row_out, col_out, deep_sem, chip_sem, core_sem
):
    me, deep, core, chip = places()
    greet(chips, deeps)
    share, piece = row_ref.shape[0], col_ref.shape[0]
    half = piece * chips
    mine = pl.ds(core * half + chip * piece, piece)
    deep_copies, chip_copies = [], []
    for o in range(1, deeps):
        deep_copies.append(
            send(
                row_ref, row_out.at[pl.ds(deep * share, share)], deep_sem, o - 1,
                {"right": lax.rem(deep + o, deeps)},
            )
        )
    for o in range(1, chips):
        chip_copies.append(
            send(
                col_ref, col_out.at[mine], chip_sem, o - 1, chip_peer(chip, core, o, chips)
            )
        )
    row_out[pl.ds(deep * share, share), :] = row_ref[...]
    col_out[mine, :] = col_ref[...]
    for copy in chip_copies:
        copy.wait()
    own = pl.ds(core * half, half)
    pair = send(
        col_out.at[own], col_out.at[own], core_sem, 0, {"left": chip * 2 + (1 - core)}
    )
    for copy in deep_copies:
        copy.wait()
    pair.wait()


def gather(row_own, col_own):
    chips, deeps = lax.axis_size("left") // 2, lax.axis_size("right")
    width = row_own.shape[1]
    return pl.pallas_call(
        functools.partial(gather_kernel, chips, deeps),
        in_specs=vmem_specs(2),
        out_specs=vmem_specs(2),
        out_shape=[
            jax.ShapeDtypeStruct((row_own.shape[0] * deeps, width), F32),
            jax.ShapeDtypeStruct((col_own.shape[0] * chips * 2, width), F32),
        ],
        scratch_shapes=[sem_pair(deeps - 1), sem_pair(chips - 1), sem_pair(1)],
        compiler_params=comm_params(2),
        name="gather",
    )(row_own, col_own)


def body(lf, rf, ld, la, rd, ra, cs, rs):
    rows, cols = lf.shape[0], rf.shape[0]
    width = cs.shape[1]
    left_n, right_n = lax.axis_size("left"), lax.axis_size("right")
    total_rows, total_cols = rows * left_n, cols * right_n
    tile, row_image, col_image = build(lf, rf, ld, la, rd, ra, cs, rs, total_rows)
    row_own, col_own = scatter(row_image, col_image)
    grams = jnp.concatenate([tdot(row_own, row_own, precise), tdot(col_own, col_own, precise)], 0)
    inverse = chol_inverse(reduce_all(grams, 3).reshape(2, width, width), True)
    row_own = apply_inverse(row_own, inverse[0], precise)
    col_own = apply_inverse(col_own, inverse[1], precise)
    grams = jnp.concatenate([tdot(row_own, row_own, precise), tdot(col_own, col_own, precise)], 0)
    inverse = chol_inverse(reduce_all(grams, 3).reshape(2, width, width), False)
    row_full, col_full = gather(row_own, col_own)
    row_part = apply_inverse(row_own, inverse[0], precise)
    col_full = apply_inverse(col_full, inverse[1], lax.Precision.HIGH)
    col_round = col_full.astype(BF16)
    applied = jnp.dot(tile, col_round, preferred_element_type=F32)
    both = jnp.concatenate([applied, applied * lf[:, None]], axis=1)
    reduced = tdot(row_full, both, lax.Precision.HIGH)
    low_rank = jnp.dot(
        lax.dot_general(row_full, ld, (((0,), (1,)), ((), ())), precision=precise),
        jnp.dot(ra, col_round.astype(F32), precision=precise) * (1.0 / total_rows),
        precision=precise,
    )
    reduced = jnp.concatenate([reduced[:, :width], reduced[:, width:] + low_rank], axis=1)
    reduced = jnp.dot(inverse[0], reduced, precision=precise)
    reduced = reduce_all(jnp.concatenate([reduced[:, :width], reduced[:, width:]], 0), 3)
    return (
        row_part * math.sqrt(total_rows),
        col_full * math.sqrt(total_cols),
        reduced[:width],
        reduced[width:],
    )


def solution(mesh):
    in_specs = (
        P("left"), P("right"), P(None, "left"), P(None, "left"),
        P(None, "right"), P(None, "right"), P("right", None), P("left", None),
    )
    out_specs = (P(("left", "right"), None), P("right", None), P(), P())
    return jax.shard_map(body, mesh=mesh, in_specs=in_specs, out_specs=out_specs, check_vma=False)
```

```python
import functools
import math

import jax
import jax.numpy as jnp
from jax import lax
from jax.experimental import pallas as pl
from jax.experimental.pallas import tpu as pltpu
from jax.sharding import PartitionSpec as P

precise = lax.Precision.HIGHEST
F32 = jnp.float32
BF16 = jnp.bfloat16
LEFT_PARTS = (0, 0, 1, 0, 1, 2)
RIGHT_PARTS = (0, 1, 0, 2, 1, 0)


def tdot(a, b, precision=None):
    return lax.dot_general(
        a, b, (((0,), (0,)), ((), ())), precision=precision, preferred_element_type=F32
    )


def split3(x):
    one = x.astype(BF16).astype(F32)
    rest = x - one
    two = rest.astype(BF16).astype(F32)
    return (one, two, (rest - two).astype(BF16).astype(F32))


def stack_parts(first, second, order):
    a, b = split3(first), split3(second)
    pieces = [a[p] for p in order] + [b[p] for p in order]
    pad = jnp.zeros((256 - 12 * first.shape[0], first.shape[1]), F32)
    return jnp.concatenate(pieces + [pad], axis=0)


def tile_kernel(
    total, rows_step,
    lf_ref, rf_ref, ld_ref, la_ref, rd_ref, ra_ref, cs_ref, rs_ref,
    tile_ref, row_ref, col_ref,
    left_scr, sketch_scr, freq_scr,
):
    step = pl.program_id(0)
    rows = left_scr.shape[0]

    @pl.when(step == 0)
    def _():
        for r in range(0, rows, 512):
            wide = jnp.broadcast_to(lf_ref[:, r:r + 512], (128, 512))
            freq_scr[r:r + 512, :] = wide.T[:, 0:1]
            stacked = stack_parts(la_ref[:, r:r + 512], -ld_ref[:, r:r + 512], LEFT_PARTS)
            left_scr[r:r + 512, :] = stacked.T.astype(BF16)
            sketch_scr[:, r:r + 512] = rs_ref[r:r + 512, :].astype(F32).T.astype(BF16)
        row_ref[...] = jnp.zeros_like(row_ref)

    right = stack_parts(rd_ref[...], ra_ref[...], RIGHT_PARTS).astype(BF16)
    freq = rf_ref[...]
    acc = jnp.zeros((256, right.shape[1]), F32)
    for chunk in range(rows // rows_step):
        sl = pl.ds(chunk * rows_step, rows_step)
        numer = jnp.dot(left_scr[sl, :], right, preferred_element_type=F32)
        gap = total * (freq_scr[sl, :] - freq)
        tile = (numer / gap).astype(BF16)
        tile_ref[sl, :] = tile
        row_ref[sl, :] += jnp.dot(tile, cs_ref[...], preferred_element_type=F32)
        acc += jnp.dot(sketch_scr[:, sl], tile, preferred_element_type=F32)
    col_ref[...] = acc.T


def build(lf, rf, ld, la, rd, ra, cs, rs, total):
    rows, cols = lf.shape[0], rf.shape[0]
    ports, width = ld.shape[0], cs.shape[1]
    tc = 256
    fixed = lambda j: (0, 0)
    return pl.pallas_call(
        functools.partial(tile_kernel, float(total), 256),
        grid=(cols // tc,),
        in_specs=[
            pl.BlockSpec((1, rows), fixed),
            pl.BlockSpec((1, tc), lambda j: (0, j)),
            pl.BlockSpec((ports, rows), fixed),
            pl.BlockSpec((ports, rows), fixed),
            pl.BlockSpec((ports, tc), lambda j: (0, j)),
            pl.BlockSpec((ports, tc), lambda j: (0, j)),
            pl.BlockSpec((tc, width), lambda j: (j, 0)),
            pl.BlockSpec((rows, width), fixed),
        ],
        out_specs=[
            pl.BlockSpec((rows, tc), lambda j: (0, j)),
            pl.BlockSpec((rows, width), fixed),
            pl.BlockSpec((tc, width), lambda j: (j, 0)),
        ],
        out_shape=[
            jax.ShapeDtypeStruct((rows, cols), BF16),
            jax.ShapeDtypeStruct((rows, width), F32),
            jax.ShapeDtypeStruct((cols, width), F32),
        ],
        scratch_shapes=[
            pltpu.VMEM((rows, 256), BF16),
            pltpu.VMEM((width, rows), BF16),
            pltpu.VMEM((rows, 1), F32),
        ],
        compiler_params=pltpu.CompilerParams(
            dimension_semantics=("arbitrary",), vmem_limit_bytes=40 << 20
        ),
        name="tiles",
    )(lf[None, :], rf[None, :], ld, la, rd, ra, cs, rs)


BLOCK = 32


def chol_kernel(shifted, g_ref, out_ref, work):
    width = g_ref.shape[-1]
    row_id = lax.broadcasted_iota(jnp.int32, (width, width), 0)
    col_id = lax.broadcasted_iota(jnp.int32, (width, width), 1)
    eye = (row_id == col_id).astype(F32)
    for m in range(2):
        gram = g_ref[m]
        if shifted:
            trace = jnp.sum(jnp.sum(gram * eye, axis=1, keepdims=True), axis=0, keepdims=True)
            gram = gram + (1e-05 * trace / width) * eye
        work[m, :, 0:width] = gram
        work[m, :, width:] = eye
    brow = lax.broadcasted_iota(jnp.int32, (BLOCK, BLOCK), 0)
    bcol = lax.broadcasted_iota(jnp.int32, (BLOCK, BLOCK), 1)
    small_eye = (brow == bcol).astype(F32)
    low = lax.broadcasted_iota(jnp.int32, (BLOCK, 2 * BLOCK), 0)
    for k in range(0, width, BLOCK):
        pairs = [
            jnp.concatenate([work[m, k:k + BLOCK, k:k + BLOCK], small_eye], axis=1)
            for m in range(2)
        ]
        for s in range(BLOCK):
            tops = [1.0 / pair[s:s + 1, s:s + 1] for pair in pairs]
            columns = [jnp.where(low > s, pair[:, s:s + 1], 0.0) for pair in pairs]
            pairs = [
                pair - column * (pair[s:s + 1, :] * top)
                for pair, column, top in zip(pairs, columns, tops)
            ]
        solved = []
        for m in range(2):
            diag = jnp.sum(pairs[m][:, 0:BLOCK] * small_eye, axis=1, keepdims=True)
            inv = pairs[m][:, BLOCK:] * lax.rsqrt(diag)
            solved.append(
                jnp.dot(
                    inv, work[m, k:k + BLOCK, :], precision=precise, preferred_element_type=F32
                )
            )
        for m in range(2):
            out_ref[m, k:k + BLOCK, :] = solved[m][:, width:]
        lo = k + BLOCK
        if lo < width:
            deltas = [tdot(rows[:, lo:width], rows, precise) for rows in solved]
            for m in range(2):
                work[m, lo:, :] = work[m, lo:, :] - deltas[m]


def chol_inverse(grams, shifted):
    width = grams.shape[-1]
    return pl.pallas_call(
        functools.partial(chol_kernel, shifted),
        in_specs=[pl.BlockSpec(memory_space=pltpu.VMEM)],
        out_specs=pl.BlockSpec(memory_space=pltpu.VMEM),
        out_shape=jax.ShapeDtypeStruct((2, width, width), F32),
        scratch_shapes=[pltpu.VMEM((2, width, 2 * width), F32)],
        compiler_params=pltpu.CompilerParams(vmem_limit_bytes=32 << 20),
        cost_estimate=pl.CostEstimate(
            flops=20_000_000_000, bytes_accessed=60_000_000, transcendentals=0
        ),
        name="factor",
    )(grams)


def apply_inverse(basis, inverse, precision):
    return lax.dot_general(
        basis, inverse, (((1,), (1,)), ((), ())), precision=precision, preferred_element_type=F32
    )


def places():
    me, deep = lax.axis_index("left"), lax.axis_index("right")
    core = lax.rem(me, 2)
    return me, deep, core, me // 2


def chip_peer(chip, core, offset, chips):
    return {"left": lax.rem(chip + offset, chips) * 2 + core}


def greet(chips, deeps):
    me, deep, core, chip = places()
    barrier = pltpu.get_barrier_semaphore()
    peers = [{"left": chip * 2 + (1 - core)}]
    peers += [chip_peer(chip, core, o, chips) for o in range(1, chips)]
    peers += [{"right": lax.rem(deep + o, deeps)} for o in range(1, deeps)]
    for peer in peers:
        pl.semaphore_signal(
            barrier, inc=1, device_id=peer, device_id_type=pl.DeviceIdType.MESH
        )
    pl.semaphore_wait(barrier, len(peers))


def send(src, dst, sems, slot, peer):
    copy = pltpu.make_async_remote_copy(
        src_ref=src,
        dst_ref=dst,
        send_sem=sems.at[0, slot],
        recv_sem=sems.at[1, slot],
        device_id=peer,
        device_id_type=pl.DeviceIdType.MESH,
    )
    copy.start()
    return copy


def scatter_kernel(
    chips, deeps, row_ref, col_ref, row_out, col_out,
    deep_buf, core_buf, half_buf, chip_buf, deep_sem, core_sem, chip_sem,
):
    me, deep, core, chip = places()
    greet(chips, deeps)
    share, half, piece = row_out.shape[0], core_buf.shape[0], col_out.shape[0]
    pair = send(
        col_ref.at[pl.ds((1 - core) * half, half)], core_buf, core_sem, 0,
        {"left": chip * 2 + (1 - core)},
    )
    deep_copies = []
    for o in range(1, deeps):
        peer = lax.rem(deep + o, deeps)
        deep_copies.append(
            send(
                row_ref.at[pl.ds(peer * share, share)], deep_buf.at[o - 1], deep_sem, o - 1,
                {"right": peer},
            )
        )
    pair.wait()

    @pl.loop(0, chips)
    def _(p):
        sl = pl.ds(p * piece, piece)
        half_buf[sl, :] = col_ref[pl.ds(core * half + p * piece, piece), :] + core_buf[sl, :]

    chip_copies = []
    for o in range(1, chips):
        peer = lax.rem(chip + o, chips)
        chip_copies.append(
            send(
                half_buf.at[pl.ds(peer * piece, piece)], chip_buf.at[o - 1], chip_sem, o - 1,
                {"left": peer * 2 + core},
            )
        )
    col_out[...] = half_buf[pl.ds(chip * piece, piece), :]
    row_out[...] = row_ref[pl.ds(deep * share, share), :]
    for o in range(1, chips):
        chip_copies[o - 1].wait()
        col_out[...] += chip_buf[o - 1]
    for o in range(1, deeps):
        deep_copies[o - 1].wait()
        row_out[...] += deep_buf[o - 1]


def vmem_specs(n):
    return [pl.BlockSpec(memory_space=pltpu.VMEM)] * n


def sem_pair(n):
    return pltpu.SemaphoreType.DMA((2, n))


def comm_params(cid):
    return pltpu.CompilerParams(
        collective_id=cid, has_side_effects=True, vmem_limit_bytes=40 << 20
    )


def scatter(row_image, col_image):
    chips, deeps = lax.axis_size("left") // 2, lax.axis_size("right")
    rows, width = row_image.shape
    cols = col_image.shape[0]
    share, half, piece = rows // deeps, cols // 2, cols // 2 // chips
    return pl.pallas_call(
        functools.partial(scatter_kernel, chips, deeps),
        in_specs=vmem_specs(2),
        out_specs=vmem_specs(2),
        out_shape=[
            jax.ShapeDtypeStruct((share, width), F32),
            jax.ShapeDtypeStruct((piece, width), F32),
        ],
        scratch_shapes=[
            pltpu.VMEM((deeps - 1, share, width), F32),
            pltpu.VMEM((half, width), F32),
            pltpu.VMEM((half, width), F32),
            pltpu.VMEM((chips - 1, piece, width), F32),
            sem_pair(deeps - 1), sem_pair(1), sem_pair(chips - 1),
        ],
        compiler_params=comm_params(1),
        name="scatter",
    )(row_image, col_image)


def reduce_kernel(
    chips, deeps, x_ref, out_ref,
    core_buf, half_buf, chip_buf, deep_buf,
    core_sem, chip_sem, deep_sem, back_sem, last_sem,
):
    me, deep, core, chip = places()
    greet(chips, deeps)
    half, piece = core_buf.shape[0], chip_buf.shape[1]
    sibling = {"left": chip * 2 + (1 - core)}
    send(x_ref.at[pl.ds((1 - core) * half, half)], core_buf, core_sem, 0, sibling).wait()
    half_buf[...] = x_ref[pl.ds(core * half, half), :] + core_buf[...]
    copies = []
    for o in range(1, chips):
        peer = lax.rem(chip + o, chips)
        copies.append(
            send(
                half_buf.at[pl.ds(peer * piece, piece)], chip_buf.at[o - 1], chip_sem, o - 1,
                {"left": peer * 2 + core},
            )
        )
    part = half_buf[pl.ds(chip * piece, piece), :]
    for o in range(1, chips):
        copies[o - 1].wait()
        part = part + chip_buf[o - 1]
    deep_buf[deep] = part
    copies = []
    for o in range(1, deeps):
        copies.append(
            send(
                deep_buf.at[deep], deep_buf.at[deep], deep_sem, o - 1,
                {"right": lax.rem(deep + o, deeps)},
            )
        )
    for copy in copies:
        copy.wait()
    part = deep_buf[0]
    for d in range(1, deeps):
        part = part + deep_buf[d]
    mine = pl.ds(core * half + chip * piece, piece)
    out_ref[mine, :] = part
    copies = []
    for o in range(1, chips):
        copies.append(
            send(
                out_ref.at[mine], out_ref.at[mine], back_sem, o - 1,
                chip_peer(chip, core, o, chips),
            )
        )
    for copy in copies:
        copy.wait()
    own = pl.ds(core * half, half)
    send(out_ref.at[own], out_ref.at[own], last_sem, 0, sibling).wait()


def reduce_all(x, cid):
    chips, deeps = lax.axis_size("left") // 2, lax.axis_size("right")
    rows, width = x.shape
    half, piece = rows // 2, rows // 2 // chips
    return pl.pallas_call(
        functools.partial(reduce_kernel, chips, deeps),
        in_specs=vmem_specs(1),
        out_specs=vmem_specs(1)[0],
        out_shape=jax.ShapeDtypeStruct(x.shape, F32),
        scratch_shapes=[
            pltpu.VMEM((half, width), F32),
            pltpu.VMEM((half, width), F32),
            pltpu.VMEM((chips - 1, piece, width), F32),
            pltpu.VMEM((deeps, piece, width), F32),
            sem_pair(1), sem_pair(chips - 1), sem_pair(deeps - 1), sem_pair(chips - 1),
            sem_pair(1),
        ],
        compiler_params=comm_params(cid),
        name="reduce",
    )(x)


def gather_kernel(chips, deeps, col_ref, col_out, chip_sem, core_sem, deep_sem):
    me, deep, core, chip = places()
    barrier = pltpu.get_barrier_semaphore()
    sibling = {"left": chip * 2 + (1 - core)}
    for peer in [sibling] + [chip_peer(chip, core, o, chips) for o in range(1, chips)]:
        pl.semaphore_signal(
            barrier, inc=1, device_id=peer, device_id_type=pl.DeviceIdType.MESH
        )
    pl.semaphore_wait(barrier, chips)
    piece = col_ref.shape[0]
    half = piece * chips
    mine = pl.ds(core * half + chip * piece, piece)
    copies = []
    for o in range(1, chips):
        copies.append(
            send(
                col_ref, col_out.at[mine], chip_sem, o - 1, chip_peer(chip, core, o, chips)
            )
        )
    pairs = [send(col_ref, col_out.at[mine], core_sem, 0, sibling)]
    col_out[mine, :] = col_ref[...]
    for o in range(1, chips):
        copies[o - 1].wait()
        came = lax.rem(chip + chips - o, chips)
        block = pl.ds(core * half + came * piece, piece)
        pairs.append(send(col_out.at[block], col_out.at[block], core_sem, o, sibling))
    for pair in pairs:
        pair.wait()


def gather(col_own):
    chips, deeps = lax.axis_size("left") // 2, lax.axis_size("right")
    width = col_own.shape[1]
    return pl.pallas_call(
        functools.partial(gather_kernel, chips, deeps),
        in_specs=vmem_specs(1),
        out_specs=vmem_specs(1)[0],
        out_shape=jax.ShapeDtypeStruct((col_own.shape[0] * chips * 2, width), F32),
        scratch_shapes=[sem_pair(chips - 1), sem_pair(chips), sem_pair(1)],
        compiler_params=comm_params(2),
        cost_estimate=pl.CostEstimate(
            flops=20_000_000_000, bytes_accessed=60_000_000, transcendentals=0
        ),
        name="gather",
    )(col_own)


def finish_kernel(scale, q_ref, inv_ref, out_ref, round_ref):
    inv = inv_ref[...]
    inv_hi = inv.astype(BF16)
    inv_lo = (inv - inv_hi.astype(F32)).astype(BF16)
    q = q_ref[...]
    q_hi = q.astype(BF16)
    q_lo = (q - q_hi.astype(F32)).astype(BF16)
    dims = (((1,), (1,)), ((), ()))
    basis = lax.dot_general(
        jnp.concatenate([q_hi, q_hi, q_lo], axis=1),
        jnp.concatenate([inv_hi, inv_lo, inv_hi], axis=1),
        dims, preferred_element_type=F32,
    )
    out_ref[...] = basis * scale
    round_ref[...] = basis.astype(BF16)


def finish(q, inverse, scale):
    rows, width = q.shape
    block = 512
    return pl.pallas_call(
        functools.partial(finish_kernel, scale),
        grid=(rows // block,),
        in_specs=[
            pl.BlockSpec((block, width), lambda i: (i, 0)),
            pl.BlockSpec((width, width), lambda i: (0, 0)),
        ],
        out_specs=[
            pl.BlockSpec((block, width), lambda i: (i, 0)),
            pl.BlockSpec((block, width), lambda i: (i, 0)),
        ],
        out_shape=[
            jax.ShapeDtypeStruct((rows, width), F32),
            jax.ShapeDtypeStruct((rows, width), BF16),
        ],
        compiler_params=pltpu.CompilerParams(dimension_semantics=("arbitrary",)),
        name="finish",
    )(q, inverse)


def body(lf, rf, ld, la, rd, ra, cs, rs):
    rows, cols = lf.shape[0], rf.shape[0]
    width = cs.shape[1]
    left_n, right_n = lax.axis_size("left"), lax.axis_size("right")
    total_rows, total_cols = rows * left_n, cols * right_n
    tile, row_image, col_image = build(lf, rf, ld, la, rd, ra, cs, rs, total_rows)
    row_own, col_own = scatter(row_image, col_image)
    grams = jnp.concatenate([tdot(row_own, row_own, precise), tdot(col_own, col_own, precise)], 0)
    inverse = chol_inverse(reduce_all(grams, 3).reshape(2, width, width), True)
    row_own = apply_inverse(row_own, inverse[0], precise)
    col_own = apply_inverse(col_own, inverse[1], precise)
    grams = jnp.concatenate([tdot(row_own, row_own, precise), tdot(col_own, col_own, precise)], 0)
    inverse = chol_inverse(reduce_all(grams, 3).reshape(2, width, width), False)
    row_full = lax.all_gather(row_own, "right", axis=0, tiled=True)
    col_full = gather(col_own)
    row_part = apply_inverse(row_own, inverse[0], precise)
    col_scaled, col_round = finish(col_full, inverse[1], math.sqrt(total_cols))
    applied = jnp.dot(tile, col_round, preferred_element_type=F32)
    both = jnp.concatenate([applied, applied * lf[:, None]], axis=1)
    reduced = tdot(row_full, both, lax.Precision.HIGH)
    low_rank = jnp.dot(
        lax.dot_general(row_full, ld, (((0,), (1,)), ((), ())), precision=precise),
        jnp.dot(ra, col_round.astype(F32), precision=precise) * (1.0 / total_rows),
        precision=precise,
    )
    reduced = jnp.concatenate([reduced[:, :width], reduced[:, width:] + low_rank], axis=1)
    reduced = jnp.dot(inverse[0], reduced, precision=precise)
    reduced = reduce_all(jnp.concatenate([reduced[:, :width], reduced[:, width:]], 0), 3)
    return (
        row_part * math.sqrt(total_rows),
        col_scaled,
        reduced[:width],
        reduced[width:],
    )


def solution(mesh):
    in_specs = (
        P("left"), P("right"), P(None, "left"), P(None, "left"),
        P(None, "right"), P(None, "right"), P("right", None), P("left", None),
    )
    out_specs = (P(("left", "right"), None), P("right", None), P(), P())
    return jax.shard_map(body, mesh=mesh, in_specs=in_specs, out_specs=out_specs, check_vma=False)
```

```python
import functools
import math

import jax
import jax.numpy as jnp
from jax import lax
from jax.experimental import pallas as pl
from jax.experimental.pallas import tpu as pltpu
from jax.sharding import PartitionSpec as P

precise = lax.Precision.HIGHEST
F32 = jnp.float32
BF16 = jnp.bfloat16
LEFT_PARTS = (0, 0, 1, 0, 1, 2)
RIGHT_PARTS = (0, 1, 0, 2, 1, 0)


def tdot(a, b, precision=None):
    return lax.dot_general(
        a, b, (((0,), (0,)), ((), ())), precision=precision, preferred_element_type=F32
    )


def split3(x):
    one = x.astype(BF16).astype(F32)
    rest = x - one
    two = rest.astype(BF16).astype(F32)
    return (one, two, (rest - two).astype(BF16).astype(F32))


def stack_parts(first, second, order):
    a, b = split3(first), split3(second)
    pieces = [a[p] for p in order] + [b[p] for p in order]
    pad = jnp.zeros((256 - 12 * first.shape[0], first.shape[1]), F32)
    return jnp.concatenate(pieces + [pad], axis=0)


def tile_kernel(
    total, rows_step,
    lf_ref, rf_ref, ld_ref, la_ref, rd_ref, ra_ref, cs_ref, rs_ref,
    tile_ref, row_ref, col_ref,
    left_scr, sketch_scr, freq_scr,
):
    step = pl.program_id(0)
    rows = left_scr.shape[0]

    @pl.when(step == 0)
    def _():
        for r in range(0, rows, 512):
            wide = jnp.broadcast_to(lf_ref[:, r:r + 512], (128, 512))
            freq_scr[r:r + 512, :] = wide.T[:, 0:1]
            stacked = stack_parts(la_ref[:, r:r + 512], -ld_ref[:, r:r + 512], LEFT_PARTS)
            left_scr[r:r + 512, :] = stacked.T.astype(BF16)
            sketch_scr[:, r:r + 512] = rs_ref[r:r + 512, :].astype(F32).T.astype(BF16)
        row_ref[...] = jnp.zeros_like(row_ref)

    right = stack_parts(rd_ref[...], ra_ref[...], RIGHT_PARTS).astype(BF16)
    freq = rf_ref[...]
    acc = jnp.zeros((256, right.shape[1]), F32)
    for chunk in range(rows // rows_step):
        sl = pl.ds(chunk * rows_step, rows_step)
        numer = jnp.dot(left_scr[sl, :], right, preferred_element_type=F32)
        gap = total * (freq_scr[sl, :] - freq)
        tile = (numer / gap).astype(BF16)
        tile_ref[sl, :] = tile
        row_ref[sl, :] += jnp.dot(tile, cs_ref[...], preferred_element_type=F32)
        acc += jnp.dot(sketch_scr[:, sl], tile, preferred_element_type=F32)
    col_ref[...] = acc.T


def build(lf, rf, ld, la, rd, ra, cs, rs, total):
    rows, cols = lf.shape[0], rf.shape[0]
    ports, width = ld.shape[0], cs.shape[1]
    tc = 256
    fixed = lambda j: (0, 0)
    return pl.pallas_call(
        functools.partial(tile_kernel, float(total), 256),
        grid=(cols // tc,),
        in_specs=[
            pl.BlockSpec((1, rows), fixed),
            pl.BlockSpec((1, tc), lambda j: (0, j)),
            pl.BlockSpec((ports, rows), fixed),
            pl.BlockSpec((ports, rows), fixed),
            pl.BlockSpec((ports, tc), lambda j: (0, j)),
            pl.BlockSpec((ports, tc), lambda j: (0, j)),
            pl.BlockSpec((tc, width), lambda j: (j, 0)),
            pl.BlockSpec((rows, width), fixed),
        ],
        out_specs=[
            pl.BlockSpec((rows, tc), lambda j: (0, j)),
            pl.BlockSpec((rows, width), fixed),
            pl.BlockSpec((tc, width), lambda j: (j, 0)),
        ],
        out_shape=[
            jax.ShapeDtypeStruct((rows, cols), BF16),
            jax.ShapeDtypeStruct((rows, width), F32),
            jax.ShapeDtypeStruct((cols, width), F32),
        ],
        scratch_shapes=[
            pltpu.VMEM((rows, 256), BF16),
            pltpu.VMEM((width, rows), BF16),
            pltpu.VMEM((rows, 1), F32),
        ],
        compiler_params=pltpu.CompilerParams(
            dimension_semantics=("arbitrary",), vmem_limit_bytes=40 << 20
        ),
        name="tiles",
    )(lf[None, :], rf[None, :], ld, la, rd, ra, cs, rs)


BLOCK = 32


def chol_kernel(shifted, g_ref, out_ref, work):
    width = g_ref.shape[-1]
    row_id = lax.broadcasted_iota(jnp.int32, (width, width), 0)
    col_id = lax.broadcasted_iota(jnp.int32, (width, width), 1)
    eye = (row_id == col_id).astype(F32)
    for m in range(2):
        gram = g_ref[m]
        if shifted:
            trace = jnp.sum(jnp.sum(gram * eye, axis=1, keepdims=True), axis=0, keepdims=True)
            gram = gram + (1e-05 * trace / width) * eye
        work[m, :, 0:width] = gram
        work[m, :, width:] = eye
    brow = lax.broadcasted_iota(jnp.int32, (BLOCK, BLOCK), 0)
    bcol = lax.broadcasted_iota(jnp.int32, (BLOCK, BLOCK), 1)
    small_eye = (brow == bcol).astype(F32)
    low = lax.broadcasted_iota(jnp.int32, (BLOCK, 2 * BLOCK), 0)
    for k in range(0, width, BLOCK):
        pairs = [
            jnp.concatenate([work[m, k:k + BLOCK, k:k + BLOCK], small_eye], axis=1)
            for m in range(2)
        ]
        for s in range(BLOCK):
            tops = [1.0 / pair[s:s + 1, s:s + 1] for pair in pairs]
            columns = [jnp.where(low > s, pair[:, s:s + 1], 0.0) for pair in pairs]
            pairs = [
                pair - column * (pair[s:s + 1, :] * top)
                for pair, column, top in zip(pairs, columns, tops)
            ]
        lo = k + BLOCK
        start, stop = k // 128 * 128, width + (lo + 127) // 128 * 128
        solved = []
        for m in range(2):
            diag = jnp.sum(pairs[m][:, 0:BLOCK] * small_eye, axis=1, keepdims=True)
            inv = pairs[m][:, BLOCK:] * lax.rsqrt(diag)
            solved.append(
                jnp.dot(
                    inv, work[m, k:lo, start:stop], precision=precise,
                    preferred_element_type=F32,
                )
            )
        for m in range(2):
            out_ref[m, k:lo, 0:stop - width] = solved[m][:, width - start:]
            if stop < 2 * width:
                out_ref[m, k:lo, stop - width:] = jnp.zeros((BLOCK, 2 * width - stop), F32)
        if lo < width:
            deltas = [tdot(rows[:, lo - start:width - start], rows, precise) for rows in solved]
            for m in range(2):
                work[m, lo:, start:stop] = work[m, lo:, start:stop] - deltas[m]


def chol_inverse(grams, shifted):
    width = grams.shape[-1]
    return pl.pallas_call(
        functools.partial(chol_kernel, shifted),
        in_specs=[pl.BlockSpec(memory_space=pltpu.VMEM)],
        out_specs=pl.BlockSpec(memory_space=pltpu.VMEM),
        out_shape=jax.ShapeDtypeStruct((2, width, width), F32),
        scratch_shapes=[pltpu.VMEM((2, width, 2 * width), F32)],
        compiler_params=pltpu.CompilerParams(vmem_limit_bytes=32 << 20),
        name="factor",
    )(grams)


def apply_inverse(basis, inverse, precision):
    return lax.dot_general(
        basis, inverse, (((1,), (1,)), ((), ())), precision=precision, preferred_element_type=F32
    )


def places():
    me, deep = lax.axis_index("left"), lax.axis_index("right")
    core = lax.rem(me, 2)
    return me, deep, core, me // 2


def chip_peer(chip, core, offset, chips):
    return {"left": lax.rem(chip + offset, chips) * 2 + core}


def greet(chips, deeps):
    me, deep, core, chip = places()
    barrier = pltpu.get_barrier_semaphore()
    peers = [{"left": chip * 2 + (1 - core)}]
    peers += [chip_peer(chip, core, o, chips) for o in range(1, chips)]
    peers += [{"right": lax.rem(deep + o, deeps)} for o in range(1, deeps)]
    for peer in peers:
        pl.semaphore_signal(
            barrier, inc=1, device_id=peer, device_id_type=pl.DeviceIdType.MESH
        )
    pl.semaphore_wait(barrier, len(peers))


def send(src, dst, sems, slot, peer):
    copy = pltpu.make_async_remote_copy(
        src_ref=src,
        dst_ref=dst,
        send_sem=sems.at[0, slot],
        recv_sem=sems.at[1, slot],
        device_id=peer,
        device_id_type=pl.DeviceIdType.MESH,
    )
    copy.start()
    return copy


def scatter_kernel(
    chips, deeps, row_ref, col_ref, row_out, col_out,
    deep_buf, core_buf, half_buf, chip_buf, deep_sem, core_sem, chip_sem,
):
    me, deep, core, chip = places()
    greet(chips, deeps)
    share, half, piece = row_out.shape[0], core_buf.shape[0], col_out.shape[0]
    pair = send(
        col_ref.at[pl.ds((1 - core) * half, half)], core_buf, core_sem, 0,
        {"left": chip * 2 + (1 - core)},
    )
    deep_copies = []
    for o in range(1, deeps):
        peer = lax.rem(deep + o, deeps)
        deep_copies.append(
            send(
                row_ref.at[pl.ds(peer * share, share)], deep_buf.at[o - 1], deep_sem, o - 1,
                {"right": peer},
            )
        )
    pair.wait()

    @pl.loop(0, chips)
    def _(p):
        sl = pl.ds(p * piece, piece)
        half_buf[sl, :] = col_ref[pl.ds(core * half + p * piece, piece), :] + core_buf[sl, :]

    chip_copies = []
    for o in range(1, chips):
        peer = lax.rem(chip + o, chips)
        chip_copies.append(
            send(
                half_buf.at[pl.ds(peer * piece, piece)], chip_buf.at[o - 1], chip_sem, o - 1,
                {"left": peer * 2 + core},
            )
        )
    col_out[...] = half_buf[pl.ds(chip * piece, piece), :]
    row_out[...] = row_ref[pl.ds(deep * share, share), :]
    for o in range(1, chips):
        chip_copies[o - 1].wait()
        col_out[...] += chip_buf[o - 1]
    for o in range(1, deeps):
        deep_copies[o - 1].wait()
        row_out[...] += deep_buf[o - 1]


def vmem_specs(n):
    return [pl.BlockSpec(memory_space=pltpu.VMEM)] * n


def sem_pair(n):
    return pltpu.SemaphoreType.DMA((2, n))


def comm_params(cid):
    return pltpu.CompilerParams(
        collective_id=cid, has_side_effects=True, vmem_limit_bytes=40 << 20
    )


def scatter(row_image, col_image):
    chips, deeps = lax.axis_size("left") // 2, lax.axis_size("right")
    rows, width = row_image.shape
    cols = col_image.shape[0]
    share, half, piece = rows // deeps, cols // 2, cols // 2 // chips
    return pl.pallas_call(
        functools.partial(scatter_kernel, chips, deeps),
        in_specs=vmem_specs(2),
        out_specs=vmem_specs(2),
        out_shape=[
            jax.ShapeDtypeStruct((share, width), F32),
            jax.ShapeDtypeStruct((piece, width), F32),
        ],
        scratch_shapes=[
            pltpu.VMEM((deeps - 1, share, width), F32),
            pltpu.VMEM((half, width), F32),
            pltpu.VMEM((half, width), F32),
            pltpu.VMEM((chips - 1, piece, width), F32),
            sem_pair(deeps - 1), sem_pair(1), sem_pair(chips - 1),
        ],
        compiler_params=comm_params(1),
        name="scatter",
    )(row_image, col_image)


def reduce_kernel(
    chips, deeps, x_ref, out_ref,
    core_buf, half_buf, chip_buf, deep_buf,
    core_sem, chip_sem, deep_sem, back_sem, last_sem,
):
    me, deep, core, chip = places()
    greet(chips, deeps)
    half, piece = core_buf.shape[0], chip_buf.shape[1]
    sibling = {"left": chip * 2 + (1 - core)}
    send(x_ref.at[pl.ds((1 - core) * half, half)], core_buf, core_sem, 0, sibling).wait()
    half_buf[...] = x_ref[pl.ds(core * half, half), :] + core_buf[...]
    copies = []
    for o in range(1, chips):
        peer = lax.rem(chip + o, chips)
        copies.append(
            send(
                half_buf.at[pl.ds(peer * piece, piece)], chip_buf.at[o - 1], chip_sem, o - 1,
                {"left": peer * 2 + core},
            )
        )
    part = half_buf[pl.ds(chip * piece, piece), :]
    for o in range(1, chips):
        copies[o - 1].wait()
        part = part + chip_buf[o - 1]
    deep_buf[deep] = part
    copies = []
    for o in range(1, deeps):
        copies.append(
            send(
                deep_buf.at[deep], deep_buf.at[deep], deep_sem, o - 1,
                {"right": lax.rem(deep + o, deeps)},
            )
        )
    for copy in copies:
        copy.wait()
    part = deep_buf[0]
    for d in range(1, deeps):
        part = part + deep_buf[d]
    mine = pl.ds(core * half + chip * piece, piece)
    out_ref[mine, :] = part
    copies = []
    for o in range(1, chips):
        copies.append(
            send(
                out_ref.at[mine], out_ref.at[mine], back_sem, o - 1,
                chip_peer(chip, core, o, chips),
            )
        )
    for copy in copies:
        copy.wait()
    own = pl.ds(core * half, half)
    send(out_ref.at[own], out_ref.at[own], last_sem, 0, sibling).wait()


def reduce_all(x, cid):
    chips, deeps = lax.axis_size("left") // 2, lax.axis_size("right")
    rows, width = x.shape
    half, piece = rows // 2, rows // 2 // chips
    return pl.pallas_call(
        functools.partial(reduce_kernel, chips, deeps),
        in_specs=vmem_specs(1),
        out_specs=vmem_specs(1)[0],
        out_shape=jax.ShapeDtypeStruct(x.shape, F32),
        scratch_shapes=[
            pltpu.VMEM((half, width), F32),
            pltpu.VMEM((half, width), F32),
            pltpu.VMEM((chips - 1, piece, width), F32),
            pltpu.VMEM((deeps, piece, width), F32),
            sem_pair(1), sem_pair(chips - 1), sem_pair(deeps - 1), sem_pair(chips - 1),
            sem_pair(1),
        ],
        compiler_params=comm_params(cid),
        name="reduce",
    )(x)


def reduce_gather_kernel(
    chips, deeps, x_ref, row_ref, col_ref, out_ref, row_out, col_out,
    core_buf, half_buf, chip_buf, deep_buf,
    core_sem, chip_sem, deep_sem, back_sem, last_sem, row_sem, col_sem, pair_sem,
):
    me, deep, core, chip = places()
    greet(chips, deeps)
    half, piece = core_buf.shape[0], chip_buf.shape[1]
    share, block = row_ref.shape[0], col_ref.shape[0]
    sibling = {"left": chip * 2 + (1 - core)}
    first = send(x_ref.at[pl.ds((1 - core) * half, half)], core_buf, core_sem, 0, sibling)
    rows_mine = pl.ds(deep * share, share)
    row_copies = []
    for o in range(1, deeps):
        row_copies.append(
            send(
                row_ref, row_out.at[rows_mine], row_sem, o - 1,
                {"right": lax.rem(deep + o, deeps)},
            )
        )
    first.wait()
    half_buf[...] = x_ref[pl.ds(core * half, half), :] + core_buf[...]
    copies = []
    for o in range(1, chips):
        peer = lax.rem(chip + o, chips)
        copies.append(
            send(
                half_buf.at[pl.ds(peer * piece, piece)], chip_buf.at[o - 1], chip_sem, o - 1,
                {"left": peer * 2 + core},
            )
        )
    cols_mine = pl.ds((core * chips + chip) * block, block)
    col_copies = []
    for o in range(1, chips):
        col_copies.append(
            send(
                col_ref, col_out.at[cols_mine], col_sem, o - 1,
                chip_peer(chip, core, o, chips),
            )
        )
    row_out[rows_mine, :] = row_ref[...]
    col_out[cols_mine, :] = col_ref[...]
    part = half_buf[pl.ds(chip * piece, piece), :]
    for o in range(1, chips):
        copies[o - 1].wait()
        part = part + chip_buf[o - 1]
    deep_buf[deep] = part
    copies = []
    for o in range(1, deeps):
        copies.append(
            send(
                deep_buf.at[deep], deep_buf.at[deep], deep_sem, o - 1,
                {"right": lax.rem(deep + o, deeps)},
            )
        )
    for copy in copies:
        copy.wait()
    part = deep_buf[0]
    for d in range(1, deeps):
        part = part + deep_buf[d]
    mine = pl.ds(core * half + chip * piece, piece)
    out_ref[mine, :] = part
    copies = []
    for o in range(1, chips):
        copies.append(
            send(
                out_ref.at[mine], out_ref.at[mine], back_sem, o - 1,
                chip_peer(chip, core, o, chips),
            )
        )
    for copy in col_copies:
        copy.wait()
    own = pl.ds(core * chips * block, chips * block)
    pair = send(col_out.at[own], col_out.at[own], pair_sem, 0, sibling)
    for copy in copies:
        copy.wait()
    own_half = pl.ds(core * half, half)
    send(out_ref.at[own_half], out_ref.at[own_half], last_sem, 0, sibling).wait()
    pair.wait()
    for copy in row_copies:
        copy.wait()


def reduce_gather(x, row_own, col_own):
    chips, deeps = lax.axis_size("left") // 2, lax.axis_size("right")
    rows, width = x.shape
    half, piece = rows // 2, rows // 2 // chips
    return pl.pallas_call(
        functools.partial(reduce_gather_kernel, chips, deeps),
        in_specs=vmem_specs(3),
        out_specs=vmem_specs(3),
        out_shape=[
            jax.ShapeDtypeStruct(x.shape, F32),
            jax.ShapeDtypeStruct((row_own.shape[0] * deeps, width), F32),
            jax.ShapeDtypeStruct((col_own.shape[0] * chips * 2, width), F32),
        ],
        scratch_shapes=[
            pltpu.VMEM((half, width), F32),
            pltpu.VMEM((half, width), F32),
            pltpu.VMEM((chips - 1, piece, width), F32),
            pltpu.VMEM((deeps, piece, width), F32),
            sem_pair(1), sem_pair(chips - 1), sem_pair(deeps - 1), sem_pair(chips - 1),
            sem_pair(1), sem_pair(deeps - 1), sem_pair(chips - 1), sem_pair(1),
        ],
        compiler_params=comm_params(2),
        name="reduce_gather",
    )(x, row_own, col_own)


def project_kernel(lf_ref, tile_ref, v_ref, q_ref, out_ref):
    @pl.when(pl.program_id(0) == 0)
    def _():
        out_ref[...] = jnp.zeros_like(out_ref)

    applied = jnp.dot(tile_ref[...], v_ref[...], preferred_element_type=F32)
    freq = jnp.broadcast_to(lf_ref[...], (128, lf_ref.shape[1])).T[:, 0:1]
    both = jnp.concatenate([applied, applied * freq], axis=1)
    both_hi = both.astype(BF16)
    both_lo = (both - both_hi.astype(F32)).astype(BF16)
    q = q_ref[...].T
    q_hi = q.astype(BF16)
    q_lo = (q - q_hi.astype(F32)).astype(BF16)
    out_ref[...] += jnp.dot(
        jnp.concatenate([q_hi, q_hi, q_lo], axis=1),
        jnp.concatenate([both_hi, both_lo, both_hi], axis=0),
        preferred_element_type=F32,
    )


def project(lf, tile, v, q):
    rows, cols = tile.shape
    width = v.shape[1]
    block = 256
    return pl.pallas_call(
        project_kernel,
        grid=(rows // block,),
        in_specs=[
            pl.BlockSpec((1, block), lambda i: (0, i)),
            pl.BlockSpec((block, cols), lambda i: (i, 0)),
            pl.BlockSpec((cols, width), lambda i: (0, 0)),
            pl.BlockSpec((block, width), lambda i: (i, 0)),
        ],
        out_specs=pl.BlockSpec((width, 2 * width), lambda i: (0, 0)),
        out_shape=jax.ShapeDtypeStruct((width, 2 * width), F32),
        compiler_params=pltpu.CompilerParams(
            dimension_semantics=("arbitrary",), vmem_limit_bytes=32 << 20
        ),
        name="project",
    )(lf[None, :], tile, v, q)


def body(lf, rf, ld, la, rd, ra, cs, rs):
    rows, cols = lf.shape[0], rf.shape[0]
    width = cs.shape[1]
    left_n, right_n = lax.axis_size("left"), lax.axis_size("right")
    total_rows, total_cols = rows * left_n, cols * right_n
    tile, row_image, col_image = build(lf, rf, ld, la, rd, ra, cs, rs, total_rows)
    row_own, col_own = scatter(row_image, col_image)
    grams = jnp.concatenate([tdot(row_own, row_own, precise), tdot(col_own, col_own, precise)], 0)
    inverse = chol_inverse(reduce_all(grams, 3).reshape(2, width, width), True)
    row_own = apply_inverse(row_own, inverse[0], precise)
    col_own = apply_inverse(col_own, inverse[1], precise)
    grams = jnp.concatenate([tdot(row_own, row_own, precise), tdot(col_own, col_own, precise)], 0)
    grams, row_full, col_full = reduce_gather(grams, row_own, col_own)
    inverse = chol_inverse(grams.reshape(2, width, width), False)
    row_part = apply_inverse(row_own, inverse[0], precise)
    col_full = apply_inverse(col_full, inverse[1], lax.Precision.HIGH)
    col_round = col_full.astype(BF16)
    reduced = project(lf, tile, col_round, row_full)
    low_rank = jnp.dot(
        lax.dot_general(row_full, ld, (((0,), (1,)), ((), ())), precision=precise),
        jnp.dot(ra, col_round.astype(F32), precision=precise) * (1.0 / total_rows),
        precision=precise,
    )
    reduced = jnp.concatenate([reduced[:, :width], reduced[:, width:] + low_rank], axis=1)
    reduced = jnp.dot(inverse[0], reduced, precision=precise)
    reduced = reduce_all(jnp.concatenate([reduced[:, :width], reduced[:, width:]], 0), 3)
    return (
        row_part * math.sqrt(total_rows),
        col_full * math.sqrt(total_cols),
        reduced[:width],
        reduced[width:],
    )


def solution(mesh):
    in_specs = (
        P("left"), P("right"), P(None, "left"), P(None, "left"),
        P(None, "right"), P(None, "right"), P("right", None), P("left", None),
    )
    out_specs = (P(("left", "right"), None), P("right", None), P(), P())
    return jax.shard_map(body, mesh=mesh, in_specs=in_specs, out_specs=out_specs, check_vma=False)
```
